512 devices in a mesh: tp: 16 (over x_hi, y), grp: 32 (over x_lo, z, core).
Axes of the slice: x: 4 (x_hi: 2, x_lo: 2; x = x_hi * 2 + x_lo), y: 8, z: 8, core: 2. Of those that a mesh axis runs over, the one named last changes fastest.
Arguments:
- low_feats: bfloat16 [1536, 16384], P('grp', 'tp'), may hold values from -40 to 40
- mid_feats: bfloat16 [1536, 16384], P('grp', 'tp'), may hold values from -40 to 40
- high_feats: bfloat16 [1536, 16384], P('grp', 'tp'), may hold values from -40 to 40
- w_low: bfloat16 [16384, 16384], P('tp', 'grp'), may hold values from -3 to 3
- w_mid: bfloat16 [16384, 16384], P('tp', 'grp'), may hold values from -3 to 3
- w_high: bfloat16 [16384, 16384], P('tp', 'grp'), may hold values from -3 to 3
- norm_gain: float32 [16384], P('grp'), may hold values from 0.1 to 1.9
- accepted: int32 [256], replicated, may hold values from 0 to 5, as said below
- assignment: int32 [256], replicated, may hold values from 0 to 255, each once
Outputs:
- drafted: bfloat16 [1536, 16384], P('tp', 'grp')
The draws below stay inside these ranges and needn't reach their ends.
Inputs may be any that keep to these rules, and one draw needn't show every extreme that they name: For every group of 8 consecutive rows starting at a multiple of 8, the sum of accepted + 1 is at most 32, and some group reaches 32; rows 2i and 2i+1 together have at most 8 positions with p <= accepted. `assignment`: each row appears once.
All inputs are finite; a program needn't handle non-finite values.
Results may differ from the reference program's by a relative error of at most 0.0008.
Values may be sent and summed in bfloat16 or wider, within the bound.
No kernel may reach another device: no remote copies, remote signals or barrier semaphores. Data moves between devices by JAX's collectives and lax.ppermute only.
A program may use at most 64 MiB of HBM per device.

```python
import math
import jax
import jax.numpy as jnp
from jax import lax

D = 16384
ROWS_G = 8
POS = 6
ROWS = 256
TOKENS = 1536


def feature_draw(key):
    key_rows, key_vals = jax.random.split(key, 2)
    row_scale = jnp.exp(jax.random.uniform(key_rows, (TOKENS, 1), jnp.float32, 0.0, math.log(10.0)))
    values = jax.random.normal(key_vals, (TOKENS, D), jnp.float32)
    values = jnp.clip(values, -4.0, 4.0)
    return (values * row_scale).astype(jnp.bfloat16)


def weight_draw(key):
    key_cols, key_vals = jax.random.split(key, 2)
    columns = jnp.arange(D, dtype=jnp.float32)
    col_scale = jnp.exp(math.log(3.0) * columns / D)[None, :]
    col_scale = col_scale * jnp.exp(jax.random.uniform(key_cols, (1, D), jnp.float32, 0.0, math.log(3.3)))
    values = jnp.clip(jax.random.normal(key_vals, (D, D), jnp.float32), -4.0, 4.0)
    return (values * col_scale * (0.5 / math.sqrt(D))).astype(jnp.bfloat16)


def draw_low_feats(key, part):
    return feature_draw(jax.random.fold_in(key, 11))


def draw_mid_feats(key, part):
    return feature_draw(jax.random.fold_in(key, 12))


def draw_high_feats(key, part):
    return feature_draw(jax.random.fold_in(key, 13))


def draw_w_low(key, part):
    return weight_draw(jax.random.fold_in(key, 21))


def draw_w_mid(key, part):
    return weight_draw(jax.random.fold_in(key, 22))


def draw_w_high(key, part):
    return weight_draw(jax.random.fold_in(key, 23))


def draw_accepted(key, part):
    key_upper, key_full, key_sums, key_split = jax.random.split(jax.random.fold_in(key, 31), 4)
    groups = ROWS // ROWS_G
    pairs = ROWS_G // 2
    group_index = jnp.arange(groups, dtype=jnp.int32)[:, None]
    upper = jax.random.randint(key_upper, (groups, 1), 2, 9)
    full_group = jax.random.randint(key_full, (), 0, groups)
    upper = jnp.where(group_index == full_group, 8, upper)
    lower = jnp.where(group_index == full_group, 8, 2)
    pair_sum = jax.random.randint(key_sums, (groups, pairs), lower, upper + 1)
    first_low = jnp.maximum(1, pair_sum - 6)
    first_high = jnp.minimum(6, pair_sum - 1)
    raw_bits = jax.random.randint(key_split, (groups, pairs), 0, 1 << 20)
    first = first_low + raw_bits % (first_high - first_low + 1)
    second = pair_sum - first
    used = jnp.stack([first, second], axis=-1).reshape(ROWS)
    return (used - 1).astype(jnp.int32)


def setup_inputs(seed: int = 0) -> dict:
    key_list = jax.random.split(jax.random.key(seed), 10)
    low_feats = draw_low_feats(jax.random.fold_in(key_list[9], 71), 0)
    mid_feats = draw_mid_feats(jax.random.fold_in(key_list[9], 71), 0)
    high_feats = draw_high_feats(jax.random.fold_in(key_list[9], 71), 0)
    w_low = draw_w_low(jax.random.fold_in(key_list[9], 71), 0)
    w_mid = draw_w_mid(jax.random.fold_in(key_list[9], 71), 0)
    w_high = draw_w_high(jax.random.fold_in(key_list[9], 71), 0)
    norm_gain = jnp.clip(1.0 + 0.18 * jax.random.normal(key_list[6], (D,), jnp.float32), 0.1, 1.9)
    accepted = draw_accepted(jax.random.fold_in(key_list[9], 71), 0)
    assignment = jax.random.permutation(key_list[8], ROWS).astype(jnp.int32)
    return dict(low_feats=low_feats, mid_feats=mid_feats, high_feats=high_feats, w_low=w_low, w_mid=w_mid, w_high=w_high, norm_gain=norm_gain, accepted=accepted, assignment=assignment)


EPSILON = 1e-05

def reference(low_feats, mid_feats, high_feats, w_low, w_mid, w_high, norm_gain, accepted, assignment):
    joined_rows = jnp.dot(low_feats, w_low, preferred_element_type=jnp.float32)
    joined_rows = joined_rows + jnp.dot(mid_feats, w_mid, preferred_element_type=jnp.float32)
    joined_rows = joined_rows + jnp.dot(high_feats, w_high, preferred_element_type=jnp.float32)
    total_tokens = accepted.shape[0] * POS
    step_index = jnp.arange(POS, dtype=jnp.int32)
    source_rows = (assignment[:, None] * POS + step_index[None, :]).reshape(total_tokens).astype(jnp.int32)
    live_rows = (step_index[None, :] <= accepted[assignment][:, None]).reshape(total_tokens)
    ordered = joined_rows[source_rows]
    squares = lax.optimization_barrier(jnp.sum(ordered * ordered, axis=1, keepdims=True))
    normed = ordered * lax.rsqrt(squares / D + EPSILON) * norm_gain[None, :]
    return jnp.where(live_rows[:, None], normed, jnp.zeros_like(normed)).astype(jnp.bfloat16)
```

```python
import jax
import jax.numpy as jnp
from jax import lax
from jax.experimental import pallas as pl
from jax.experimental.pallas import tpu as pltpu
from jax.sharding import Mesh
from jax.sharding import PartitionSpec as P

D = 16384
ROWS_G = 8
POS = 6
SLOTS = 8
EPSILON = 1e-05
TP = ("xh", "y")
GRP = ("xl", "z", "c")
SWAP = [(0, 1), (1, 0)]


def both_ways(n):
    pairs = []
    for i in range(n):
        for c in range(2):
            to = (i + (1 if c == 0 else n - 1)) % n
            pairs.append((i * 2 + c, to * 2 + c))
    return pairs


def diagonal(n):
    pairs = []
    for x in range(2):
        for i in range(n):
            for c in range(2):
                to = (i + (1 if c == 0 else n - 1)) % n
                pairs.append(((x * n + i) * 2 + c, ((1 - x) * n + to) * 2 + c))
    return pairs


def shifted(n, by):
    return [(i, (i + by) % n) for i in range(n)]


def crossing(n, by):
    return [(x * n + i, (1 - x) * n + (i + by) % n) for x in range(2) for i in range(n)]


def other_core(x):
    return lax.ppermute(x, "c", SWAP)


def onward(x, axis):
    return lax.ppermute(x, (axis, "c"), both_ways(lax.axis_size(axis)))


def project(x, weights):
    k = weights[0].shape[0]
    total = jnp.dot(x[:, :k], weights[0], preferred_element_type=jnp.float32)
    for i in (1, 2):
        total = total + jnp.dot(
            x[:, i * k : (i + 1) * k], weights[i], preferred_element_type=jnp.float32
        )
    return total


def pick_kernel(group, accepted, low, mid, high, out):
    slots, tokens = out.shape[0], low.shape[0]
    slot = lax.broadcasted_iota(jnp.int32, (slots, tokens), 0)
    token = lax.broadcasted_iota(jnp.int32, (slots, tokens), 1)
    pair, at = slot // SLOTS, slot % SLOTS
    used = jnp.zeros_like(slot)
    for i in range(ROWS_G // 2):
        used = jnp.where(pair == i, accepted[group[0] * ROWS_G + 2 * i] + 1, used)
    source = pair * (2 * POS) + jnp.where(at < used, at, 2 * POS + 1 - at)
    pick = jnp.where(source == token, 1.0, 0.0).astype(jnp.bfloat16)
    k = low.shape[1]
    for i, feats in enumerate((low, mid, high)):
        out[:, i * k : (i + 1) * k] = jnp.dot(
            pick, feats[...], preferred_element_type=jnp.float32
        ).astype(jnp.bfloat16)


def selected(feats, group, accepted):
    smem, vmem = pl.BlockSpec(memory_space=pltpu.SMEM), pl.BlockSpec(memory_space=pltpu.VMEM)
    return pl.pallas_call(
        pick_kernel,
        out_shape=jax.ShapeDtypeStruct(
            (ROWS_G // 2 * SLOTS, 3 * feats[0].shape[1]), jnp.bfloat16
        ),
        in_specs=[smem, smem, vmem, vmem, vmem],
        out_specs=vmem,
        name="pick",
    )(group[None], accepted, *feats)


def per_device(
    low_feats, mid_feats, high_feats, w_low, w_mid, w_high, norm_gain, accepted, assignment
):
    weights = (w_low, w_mid, w_high)
    xh, y, xl, z, c = (lax.axis_index(a) for a in ("xh", "y", "xl", "z", "c"))
    ny, nz = lax.axis_size("y"), lax.axis_size("z")
    way = 1 - 2 * c
    group = (xl * nz + z) * 2 + c
    mine = selected((low_feats, mid_feats, high_feats), group, accepted)
    block = mine.shape[0]

    chip = jnp.concatenate([mine, other_core(mine)], 0)
    beside = lax.ppermute(mine, "xl", SWAP)
    straight = [onward(chip, "z")]
    crossed = [lax.ppermute(chip, GRP, diagonal(nz))]
    for s in (2, 3):
        straight.append(onward(straight[-1], "z"))
        crossed.append(onward(crossed[-1], "z"))
    last = [onward(straight[-1][:block], "z"), onward(crossed[-1][:block], "z")]
    early = jnp.concatenate([straight[0], crossed[0], straight[1], crossed[1], beside], 0)
    early, _ = lax.optimization_barrier((early, straight[2]))
    there_early = other_core(early)
    late = jnp.concatenate([straight[2], crossed[2]], 0)
    there_late = other_core(late)
    last = jnp.concatenate(last, 0)
    there_last = other_core(last)
    cut = 8 * block
    pieces = [
        chip,
        jnp.concatenate([beside, there_early[cut:]], 0),
        early[:cut],
        there_early[:cut],
        late,
        there_late,
        last,
        there_last,
    ]
    partial_value = jnp.concatenate([project(p, weights) for p in pieces], 0)

    slabs, per_slab = 2 * ny, assignment.shape[0] // (2 * ny)
    own_target = lax.dynamic_slice(assignment, ((xh * ny + y) * per_slab,), (per_slab,))
    target, _ = lax.optimization_barrier((assignment, straight[0]))
    target = target.reshape(2, ny, per_slab)
    target = lax.dynamic_slice(
        jnp.concatenate([target, target, target], 1),
        (0, y + ny // 2, 0),
        (2, ny, per_slab),
    )
    target = jnp.where(xh == 0, target[::-1], target).transpose(1, 0, 2).reshape(-1)
    of_group = target // ROWS_G
    there_c, there_z, there_x = of_group % 2, (of_group // 2) % nz, of_group // (2 * nz)
    dx, dc, dz = there_x ^ xl, there_c ^ c, (there_z - z) % nz
    step = (-way * dz) % nz
    near = jnp.minimum(step, nz - step)
    from_here = step < nz // 2
    place = jnp.where(
        near == 0,
        dx * 2 + dc,
        jnp.where(
            near == nz // 2,
            28 + dc * 2 + dx,
            jnp.where(near == 3, 20, near * 4)
            + jnp.where(from_here, dx * 2 + dc, jnp.where(near == 3, 5, 9) + dx * 2 - dc),
        ),
    )
    in_group = target % ROWS_G
    even = in_group % 2 == 0
    first = place * block + (in_group // 2) * SLOTS + jnp.where(even, 0, SLOTS - 1)
    position = jnp.arange(POS, dtype=jnp.int32)
    token = (
        first[:, None] + jnp.where(even, 1, -1)[:, None] * position[None, :]
    ).reshape(-1)
    size = per_slab * POS

    ahead, back = shifted(ny, 1), shifted(ny, ny - 1)
    far = partial_value[token[: 2 * size]]
    rest = partial_value[token[2 * size :]]

    def rows(k):
        at = ((k + ny // 2) % ny - 1) * 2 * size
        return rest[at : at + 2 * size]

    up = lax.ppermute(far[:size], "y", ahead)
    down = lax.ppermute(far[size:], "y", back)
    own = rows(0)
    across = lax.ppermute(own[:size], "xh", SWAP)
    none = jnp.zeros_like(up)
    up = rows(3) + jnp.concatenate([up, none], 0)
    up = lax.ppermute(up, "y", ahead)
    down = rows(-3) + jnp.concatenate([none, down], 0)
    down = lax.ppermute(down, "y", back)
    up = lax.ppermute(lax.optimization_barrier(up + rows(2)), "y", ahead)
    down = lax.ppermute(lax.optimization_barrier(down + rows(-2)), "y", back)
    up = lax.optimization_barrier(up + rows(1))
    down = lax.optimization_barrier(down + rows(-1))
    summed = (
        own[size:]
        + across
        + lax.ppermute(up[:size], TP, crossing(ny, 1))
        + lax.ppermute(up[size:], "y", ahead)
        + lax.ppermute(down[:size], TP, crossing(ny, ny - 1))
        + lax.ppermute(down[size:], "y", back)
    )

    squares = jnp.sum(summed * summed, axis=1)
    squares = jnp.sum(
        lax.all_to_all(
            jnp.broadcast_to(squares[None], (4 * nz, size)), GRP, 0, 0, tiled=True
        ),
        axis=0,
    )
    inverse = lax.rsqrt(squares / D + EPSILON)
    normed = summed * inverse[:, None] * norm_gain[None, :]
    own_used = jnp.sum(
        jnp.where(
            own_target[:, None] == jnp.arange(accepted.shape[0], dtype=jnp.int32)[None, :],
            accepted[None, :],
            0,
        ),
        axis=1,
    )
    live = (position[None, :] <= own_used[:, None]).reshape(size)
    return jnp.where(live[:, None], normed, jnp.zeros_like(normed)).astype(jnp.bfloat16)


def solution(mesh):
    split = Mesh(mesh.devices.reshape(2, 8, 2, 8, 2), ("xh", "y", "xl", "z", "c"))
    feats, weight = P(GRP, TP), P(TP, GRP)
    return jax.shard_map(
        per_device,
        mesh=split,
        in_specs=(feats, feats, feats, weight, weight, weight, P(GRP), P(), P()),
        out_specs=P(TP, GRP),
        check_vma=False,
    )
```

```python
import jax
import jax.numpy as jnp
from jax import lax
from jax.experimental import pallas as pl
from jax.experimental.pallas import tpu as pltpu
from jax.sharding import Mesh
from jax.sharding import PartitionSpec as P

D = 16384
ROWS_G = 8
POS = 6
SLOTS = 8
EPSILON = 1e-05
TP = ("xh", "y")
GRP = ("xl", "z", "c")
SWAP = [(0, 1), (1, 0)]


def both_ways(n):
    pairs = []
    for i in range(n):
        for c in range(2):
            to = (i + (1 if c == 0 else n - 1)) % n
            pairs.append((i * 2 + c, to * 2 + c))
    return pairs


def diagonal(n):
    pairs = []
    for x in range(2):
        for i in range(n):
            for c in range(2):
                to = (i + (1 if c == 0 else n - 1)) % n
                pairs.append(((x * n + i) * 2 + c, ((1 - x) * n + to) * 2 + c))
    return pairs


def other_core(x):
    return lax.ppermute(x, "c", SWAP)


def onward(x, axis):
    return lax.ppermute(x, (axis, "c"), both_ways(lax.axis_size(axis)))


VMEM = pl.BlockSpec(memory_space=pltpu.VMEM)
SMEM = pl.BlockSpec(memory_space=pltpu.SMEM)
SMALL = pltpu.CompilerParams(vmem_limit_bytes=8 << 20)


def joined(*parts):
    def kernel(*refs):
        at = 0
        for ref in refs[:-1]:
            refs[-1][at : at + ref.shape[0]] = ref[...]
            at += ref.shape[0]

    shape = (sum(p.shape[0] for p in parts), *parts[0].shape[1:])
    return pl.pallas_call(
        kernel,
        out_shape=jax.ShapeDtypeStruct(shape, parts[0].dtype),
        in_specs=[VMEM] * len(parts),
        out_specs=VMEM,
        compiler_params=SMALL,
        name="joined",
    )(*parts)


def each_row(me, first, turn, values, block, do):
    xh, y, c, ny = me[0], me[1], me[2], 8
    k, v = block // 2 - 4, block % 2
    if k == -4:
        h = jnp.where(c == v, 1 - xh, xh)
    else:
        h = xh if v else 1 - xh
    slab = h * ny + lax.rem(y + (1 - 2 * c) * k + ny, ny)
    per_slab = first.shape[0] // (2 * ny)

    @pl.loop(0, per_slab)
    def _(i):
        start, by = first[slab * per_slab + i], turn[slab * per_slab + i]
        for p in range(POS):
            do(i * POS + p, values[pl.ds(start + by * p, 1), :])


def taken(table, blocks):
    _, first, _, values = table

    def kernel(me, first, turn, values, out):
        for n, block in enumerate(blocks):

            def store(r, row, n=n):
                out[n, pl.ds(r, 1), :] = row

            each_row(me, first, turn, values, block, store)

    return pl.pallas_call(
        kernel,
        out_shape=jax.ShapeDtypeStruct(
            (len(blocks), first.shape[0] // 16 * POS, values.shape[1]), values.dtype
        ),
        in_specs=[SMEM, SMEM, SMEM, VMEM],
        out_specs=VMEM,
        compiler_params=SMALL,
        name="taken",
    )(*table)


def paired(table, block, theirs, at, came=None, first_step=False):
    def kernel(*refs):
        me, first, turn, values, theirs = refs[:5]
        out = refs[-1]

        def store(r, row):
            out[0, pl.ds(r, 1), :] = row

        each_row(me, first, turn, values, block, store)
        if came is None:
            out[1] = theirs[at]
        elif not first_step:
            out[0] = out[0] + refs[5][0]
            out[1] = theirs[at] + refs[5][1]
        else:
            wanted = me[2] == block % 2
            out[0] = out[0] + jnp.where(wanted, refs[5][0], 0.0)
            out[1] = theirs[at] + jnp.where(wanted, refs[5][1], 0.0)

    more = [] if came is None else [came]
    return pl.pallas_call(
        kernel,
        out_shape=jax.ShapeDtypeStruct((2, *theirs.shape[1:]), theirs.dtype),
        in_specs=[SMEM, SMEM, SMEM, VMEM, VMEM, VMEM][: 5 + len(more)],
        out_specs=VMEM,
        compiler_params=SMALL,
        name="paired",
    )(*table, theirs, *more)


def pick_kernel(group, accepted, low, mid, high, out, used_by, held, sems):
    feats = (low, mid, high)
    copies = [pltpu.make_async_copy(accepted, used_by, sems.at[3])]
    copies += [pltpu.make_async_copy(f, held.at[i], sems.at[i]) for i, f in enumerate(feats)]
    for copy in copies:
        copy.start()
    slots, (tokens, k) = out.shape[0], low.shape
    slot = lax.broadcasted_iota(jnp.int32, (slots, tokens), 0)
    token = lax.broadcasted_iota(jnp.int32, (slots, tokens), 1)
    pair, at = slot // SLOTS, slot % SLOTS
    used = jnp.zeros_like(slot)
    copies[0].wait()
    for i in range(ROWS_G // 2):
        used = jnp.where(pair == i, used_by[group[0] * ROWS_G + 2 * i] + 1, used)
    source = pair * (2 * POS) + jnp.where(at < used, at, 2 * POS + 1 - at)
    pick = jnp.where(source == token, 1.0, 0.0).astype(jnp.bfloat16)
    for i in range(3):
        copies[1 + i].wait()
        out[:, i * k : (i + 1) * k] = jnp.dot(
            pick, held[i], preferred_element_type=jnp.float32
        ).astype(jnp.bfloat16)


def selected(feats, group, accepted):
    slots, width = ROWS_G // 2 * SLOTS, 3 * feats[0].shape[1]
    return pl.pallas_call(
        pick_kernel,
        out_shape=jax.ShapeDtypeStruct((slots, width), jnp.bfloat16),
        in_specs=[SMEM] + [pl.BlockSpec(memory_space=pl.ANY)] * 4,
        out_specs=VMEM,
        scratch_shapes=[
            pltpu.SMEM(accepted.shape, jnp.int32),
            pltpu.VMEM((3, *feats[0].shape), jnp.bfloat16),
            pltpu.SemaphoreType.DMA((4,)),
        ],
        compiler_params=pltpu.CompilerParams(vmem_limit_bytes=60 << 20),
        name="pick",
    )(group[None], accepted, *feats)


def product(parts, weights, rows, at, before=None):
    k, columns = weights[0].shape
    count = sum(n for _, _, n in parts)

    arrays = []
    for p, _, _ in parts:
        if not any(p is q for q in arrays):
            arrays.append(p)
    which = [next(i for i, q in enumerate(arrays) if q is p) for p, _, _ in parts]

    def kernel(*refs):
        n = len(arrays)
        ws, out, held = refs[n : n + 3], refs[-2], refs[-1]
        to = 0
        for i, (_, start, number) in zip(which, parts, strict=True):
            held[to : to + number] = refs[i][start : start + number]
            to += number
        total = jnp.dot(held[:, :k], ws[0][...], preferred_element_type=jnp.float32)
        for i in (1, 2):
            total += jnp.dot(
                held[:, i * k : (i + 1) * k], ws[i][...], preferred_element_type=jnp.float32
            )
        out[at : at + count] = total

    operands = arrays + list(weights)
    aliases = {} if before is None else {len(operands): 0}
    return pl.pallas_call(
        kernel,
        out_shape=jax.ShapeDtypeStruct((rows, columns), jnp.float32),
        in_specs=[VMEM] * (len(operands) + len(aliases)),
        out_specs=VMEM,
        scratch_shapes=[pltpu.VMEM((count, 3 * k), jnp.bfloat16)],
        input_output_aliases=aliases,
        compiler_params=pltpu.CompilerParams(vmem_limit_bytes=12 << 20),
        name="product",
    )(*operands, *([] if before is None else [before]))


def step_on_device(
    low_feats, mid_feats, high_feats, w_low, w_mid, w_high, norm_gain, accepted, assignment
):
    weights = (w_low, w_mid, w_high)
    xh, y, xl, z, c = (lax.axis_index(a) for a in ("xh", "y", "xl", "z", "c"))
    ny, nz = lax.axis_size("y"), lax.axis_size("z")
    way = 1 - 2 * c
    group = (xl * nz + z) * 2 + c
    mine = selected((low_feats, mid_feats, high_feats), group, accepted)
    block = mine.shape[0]

    chip = joined(mine, other_core(mine))
    straight = [onward(chip, "z")]
    crossed = [lax.ppermute(chip, GRP, diagonal(nz))]
    beside = lax.ppermute(mine, "xl", SWAP)
    for _ in range(2):
        straight.append(onward(straight[-1], "z"))
        crossed.append(onward(crossed[-1], "z"))
    straight.append(onward(straight[-1][:block], "z"))
    crossed.append(onward(crossed[-1][:block], "z"))
    here, there = [], []
    for s in range(4):
        here.append(joined(straight[s], crossed[s], *((beside,) if s == 1 else ())))
        there.append(other_core(here[s]))
    cut = 4 * block
    total = 32 * block
    partial_value = product([(chip, 0, 2 * block)], weights, total, 0)
    parts = [
        (beside, 0, block),
        (there[1], cut, block),
        (here[0], 0, cut),
        (there[0], 0, cut),
        (here[1], 0, cut),
        (there[1], 0, cut),
    ]
    partial_value = product(parts, weights, total, 2 * block, partial_value)
    parts = [
        (here[2], 0, cut),
        (there[2], 0, cut),
        (here[3], 0, 2 * block),
        (there[3], 0, 2 * block),
    ]
    partial_value = product(parts, weights, total, 20 * block, partial_value)

    per_slab = assignment.shape[0] // (2 * ny)
    target = assignment
    of_group = target // ROWS_G
    there_c, there_z, there_x = of_group % 2, (of_group // 2) % nz, of_group // (2 * nz)
    dx, dc, dz = there_x ^ xl, there_c ^ c, (there_z - z) % nz
    step = (-way * dz) % nz
    near = jnp.minimum(step, nz - step)
    from_here = step < nz // 2
    place = jnp.where(
        near == 0,
        dx * 2 + dc,
        jnp.where(
            near == nz // 2,
            28 + dc * 2 + dx,
            near * 8 - 4 + jnp.where(from_here, dx * 2 + dc, 5 + dx * 2 - dc),
        ),
    )
    in_group = target % ROWS_G
    even = in_group % 2 == 0
    first = place * block + (in_group // 2) * SLOTS + jnp.where(even, 0, SLOTS - 1)
    turn = jnp.where(even, 1, -1)
    size = per_slab * POS

    table = (jnp.stack([xh, y, c]), first, turn, partial_value)
    far = taken(table, (1,))
    behind = taken(table, tuple(range(2, 8)))
    beyond = taken(table, (8,))[0]
    own = taken(table, (9,))[0]
    far = paired(table, 0, other_core(far), 0)
    far = onward(far, "y")
    behind = other_core(behind)
    across = lax.ppermute(beyond, "xh", SWAP)
    came = [far, far]
    for step, k in enumerate((3, 2, 1)):
        for v in range(2):
            total = paired(
                table, 8 + 2 * k + v, behind, 2 * step + v, came[v], step == 0
            )
            if k == 1 and v == 0:
                came[v] = lax.ppermute(total, (*TP, "c"), diagonal(ny))
            else:
                came[v] = onward(total, "y")
    given = other_core(came[0][1] + came[1][1])
    summed = own + across + came[0][0] + came[1][0] + given

    squares = jnp.sum(summed * summed, axis=1)
    squares = jnp.sum(
        lax.all_to_all(
            jnp.broadcast_to(squares[None], (4 * nz, size)), GRP, 0, 0, tiled=True
        ),
        axis=0,
    )
    inverse = lax.rsqrt(squares / D + EPSILON)
    own_target = lax.dynamic_slice(target, ((xh * ny + y) * per_slab,), (per_slab,))
    own_used = jnp.sum(
        jnp.where(
            own_target[:, None] == jnp.arange(accepted.shape[0], dtype=jnp.int32)[None, :],
            accepted[None, :],
            0,
        ),
        axis=1,
    )
    live = (jnp.arange(POS, dtype=jnp.int32)[None, :] <= own_used[:, None]).reshape(size)
    normed = summed * inverse[:, None] * norm_gain[None, :]
    return jnp.where(live[:, None], normed, jnp.zeros_like(normed)).astype(jnp.bfloat16)


def solution(mesh):
    split = Mesh(mesh.devices.reshape(2, 8, 2, 8, 2), ("xh", "y", "xl", "z", "c"))
    feats, weight = P(GRP, TP), P(TP, GRP)
    return jax.shard_map(
        step_on_device,
        mesh=split,
        in_specs=(feats, feats, feats, weight, weight, weight, P(GRP), P(), P()),
        out_specs=P(TP, GRP),
        check_vma=False,
    )
```

```python
import jax
import jax.numpy as jnp
from jax import lax
from jax.experimental import pallas as pl
from jax.experimental.pallas import tpu as pltpu
from jax.sharding import Mesh
from jax.sharding import PartitionSpec as P

D = 16384
ROWS_G = 8
POS = 6
SLOTS = 8
EPSILON = 1e-05
TP = ("xh", "y")
GRP = ("xl", "z", "c")
SWAP = [(0, 1), (1, 0)]


def both_ways(n):
    pairs = []
    for i in range(n):
        for c in range(2):
            to = (i + (1 if c == 0 else n - 1)) % n
            pairs.append((i * 2 + c, to * 2 + c))
    return pairs


def diagonal(n):
    pairs = []
    for x in range(2):
        for i in range(n):
            for c in range(2):
                to = (i + (1 if c == 0 else n - 1)) % n
                pairs.append(((x * n + i) * 2 + c, ((1 - x) * n + to) * 2 + c))
    return pairs


def other_core(x):
    return lax.ppermute(x, "c", SWAP)


def onward(x, axis):
    return lax.ppermute(x, (axis, "c"), both_ways(lax.axis_size(axis)))


VMEM = pl.BlockSpec(memory_space=pltpu.VMEM)
SMEM = pl.BlockSpec(memory_space=pltpu.SMEM)
HBM = pl.BlockSpec(memory_space=pltpu.HBM)
SMALL = pltpu.CompilerParams(vmem_limit_bytes=8 << 20)


def joined(*parts):
    def kernel(*refs):
        at = 0
        for ref in refs[:-1]:
            refs[-1][at : at + ref.shape[0]] = ref[...]
            at += ref.shape[0]

    shape = (sum(p.shape[0] for p in parts), *parts[0].shape[1:])
    return pl.pallas_call(
        kernel,
        out_shape=jax.ShapeDtypeStruct(shape, parts[0].dtype),
        in_specs=[VMEM] * len(parts),
        out_specs=VMEM,
        compiler_params=SMALL,
        name="joined",
    )(*parts)


def upper(x, rows):
    def kernel(x, out):
        out[...] = x[:rows]

    return pl.pallas_call(
        kernel,
        out_shape=jax.ShapeDtypeStruct((rows, x.shape[1]), x.dtype),
        in_specs=[VMEM],
        out_specs=VMEM,
        compiler_params=SMALL,
        name="upper",
    )(x)


def each_row(me, first, turn, values, block, do):
    xh, y, c, ny = me[0], me[1], me[2], 8
    k, v = block // 2 - 4, block % 2
    if k == -4:
        h = jnp.where(c == v, 1 - xh, xh)
    else:
        h = xh if v else 1 - xh
    slab = h * ny + lax.rem(y + (1 - 2 * c) * k + ny, ny)
    per_slab = first.shape[0] // (2 * ny)

    @pl.loop(0, per_slab)
    def _(i):
        start, by = first[slab * per_slab + i], turn[slab * per_slab + i]
        for p in range(POS):
            do(i * POS + p, values[pl.ds(start + by * p, 1), :])


def taken(table, blocks):
    _, first, _, values = table

    def kernel(me, first, turn, values, out):
        for n, block in enumerate(blocks):

            def store(r, row, n=n):
                out[n, pl.ds(r, 1), :] = row

            each_row(me, first, turn, values, block, store)

    return pl.pallas_call(
        kernel,
        out_shape=jax.ShapeDtypeStruct(
            (len(blocks), first.shape[0] // 16 * POS, values.shape[1]), values.dtype
        ),
        in_specs=[SMEM, SMEM, SMEM, VMEM],
        out_specs=VMEM,
        compiler_params=SMALL,
        name="taken",
    )(*table)


def paired(table, block, theirs, at, came=None, first_step=False):
    def kernel(*refs):
        me, first, turn, values, theirs = refs[:5]
        out = refs[-1]

        def store(r, row):
            out[0, pl.ds(r, 1), :] = row

        each_row(me, first, turn, values, block, store)
        if came is None:
            out[1] = theirs[at]
        elif not first_step:
            out[0] = out[0] + refs[5][0]
            out[1] = theirs[at] + refs[5][1]
        else:
            wanted = me[2] == block % 2
            out[0] = out[0] + jnp.where(wanted, refs[5][0], 0.0)
            out[1] = theirs[at] + jnp.where(wanted, refs[5][1], 0.0)

    more = [] if came is None else [came]
    return pl.pallas_call(
        kernel,
        out_shape=jax.ShapeDtypeStruct((2, *theirs.shape[1:]), theirs.dtype),
        in_specs=[SMEM, SMEM, SMEM, VMEM, VMEM, VMEM][: 5 + len(more)],
        out_specs=VMEM,
        compiler_params=SMALL,
        name="paired",
    )(*table, theirs, *more)


def pick_kernel(me, accepted, low, mid, high, out, used_by, held, sems):
    feats = (low, mid, high)
    copies = [pltpu.make_async_copy(accepted, used_by, sems.at[3])]
    copies += [pltpu.make_async_copy(f, held.at[i], sems.at[i]) for i, f in enumerate(feats)]
    for copy in copies:
        copy.start()
    slots, (tokens, k) = out.shape[0], low.shape
    slot = lax.broadcasted_iota(jnp.int32, (slots, tokens), 0)
    token = lax.broadcasted_iota(jnp.int32, (slots, tokens), 1)
    pair, at = slot // SLOTS, slot % SLOTS
    used = jnp.zeros_like(slot)
    copies[0].wait()
    for i in range(ROWS_G // 2):
        used = jnp.where(pair == i, used_by[me[3] * ROWS_G + 2 * i] + 1, used)
    source = pair * (2 * POS) + jnp.where(at < used, at, 2 * POS + 1 - at)
    pick = jnp.where(source == token, 1.0, 0.0).astype(jnp.bfloat16)
    for i in range(3):
        copies[1 + i].wait()
        out[:, i * k : (i + 1) * k] = jnp.dot(
            pick, held[i], preferred_element_type=jnp.float32
        ).astype(jnp.bfloat16)


def selected(feats, me, accepted):
    slots, width = ROWS_G // 2 * SLOTS, 3 * feats[0].shape[1]
    return pl.pallas_call(
        pick_kernel,
        out_shape=jax.ShapeDtypeStruct((slots, width), jnp.bfloat16),
        in_specs=[SMEM] + [HBM] * 4,
        out_specs=VMEM,
        scratch_shapes=[
            pltpu.SMEM(accepted.shape, jnp.int32),
            pltpu.VMEM((3, *feats[0].shape), jnp.bfloat16),
            pltpu.SemaphoreType.DMA((4,)),
        ],
        compiler_params=SMALL,
        name="pick",
    )(me, *(pltpu.with_memory_space_constraint(x, pltpu.HBM) for x in (accepted, *feats)))


def product(parts, weights, rows, at, before=None):
    columns = weights[0].shape[1]
    count = sum(n for _, _, n in parts)
    arrays = []
    for p, _, _ in parts:
        if not any(p is q for q in arrays):
            arrays.append(p)
    which = [next(i for i, q in enumerate(arrays) if q is p) for p, _, _ in parts]
    depth = arrays[0].shape[1]

    def kernel(*refs):
        n = len(arrays)
        if before is None:
            out, near, held, sems = refs[-4:]
            k = depth // 3
            copies = [
                pltpu.make_async_copy(refs[n + i], near.at[pl.ds(i * k, k)], sems.at[i])
                for i in range(3)
            ]
            for copy in copies:
                copy.start()
        else:
            near, (out, _, held) = refs[n], refs[-3:]
        to = 0
        for i, (_, start, number) in zip(which, parts, strict=True):
            held[to : to + number] = refs[i][start : start + number]
            to += number
        if before is None:
            for copy in copies:
                copy.wait()
        out[at : at + count] = jnp.dot(
            held[...], near[...], preferred_element_type=jnp.float32
        )

    if before is None:
        weights = [pltpu.with_memory_space_constraint(w, pltpu.HBM) for w in weights]
    operands = arrays + list(weights)
    aliases = {} if before is None else {len(operands): 0, len(arrays): 1}
    shapes = (
        jax.ShapeDtypeStruct((rows, columns), jnp.float32),
        jax.ShapeDtypeStruct((depth, columns), jnp.bfloat16),
    )
    return pl.pallas_call(
        kernel,
        out_shape=shapes,
        in_specs=[VMEM] * len(arrays) + ([HBM] * 3 if before is None else [VMEM] * 2),
        out_specs=(VMEM,) * len(shapes),
        scratch_shapes=[pltpu.VMEM((count, depth), jnp.bfloat16)]
        + ([pltpu.SemaphoreType.DMA((3,))] if before is None else []),
        input_output_aliases=aliases,
        compiler_params=pltpu.CompilerParams(vmem_limit_bytes=6 << 20),
        name="product",
    )(*operands, *([] if before is None else [before]))


def step_on_device(
    low_feats, mid_feats, high_feats, w_low, w_mid, w_high, norm_gain, accepted, assignment
):
    weights = (w_low, w_mid, w_high)
    xh, y, xl, z, c = (lax.axis_index(a) for a in ("xh", "y", "xl", "z", "c"))
    ny, nz = lax.axis_size("y"), lax.axis_size("z")
    way = 1 - 2 * c
    group = (xl * nz + z) * 2 + c
    me = lax.optimization_barrier(jnp.stack([xh, y, c, group, xl, z, way]))
    mine = selected((low_feats, mid_feats, high_feats), me, accepted)
    block = mine.shape[0]

    chip = joined(mine, other_core(mine))
    straight = [onward(chip, "z")]
    crossed = [lax.ppermute(chip, GRP, diagonal(nz))]
    beside = lax.ppermute(mine, "xl", SWAP)
    for _ in range(2):
        straight.append(onward(straight[-1], "z"))
        crossed.append(onward(crossed[-1], "z"))
    half = upper(straight[-1], block)
    straight.append(onward(half, "z"))
    half = upper(crossed[-1], block)
    crossed.append(onward(half, "z"))
    here, there = [], []
    for s in range(4):
        here.append(joined(straight[s], crossed[s], *((beside,) if s == 1 else ())))
        there.append(other_core(here[s]))
    cut = 4 * block
    total = 32 * block
    partial_value, near = product([(chip, 0, 2 * block)], weights, total, 0)
    parts = [
        (beside, 0, block),
        (there[1], cut, block),
        (here[0], 0, cut),
        (there[0], 0, cut),
        (here[1], 0, cut),
        (there[1], 0, cut),
    ]
    partial_value, near = product(parts, (near,), total, 2 * block, partial_value)
    parts = [(here[2], 0, cut), (there[2], 0, cut)]
    partial_value, near = product(parts, (near,), total, 20 * block, partial_value)
    parts = [(here[3], 0, 2 * block), (there[3], 0, 2 * block)]
    partial_value, near = product(parts, (near,), total, 28 * block, partial_value)

    per_slab = assignment.shape[0] // (2 * ny)
    target = assignment
    of_group = target // ROWS_G
    there_c, there_z, there_x = of_group % 2, (of_group // 2) % nz, of_group // (2 * nz)
    dx, dc, dz = there_x ^ me[4], there_c ^ me[2], (there_z - me[5]) % nz
    step = (nz - me[6] * dz) % nz
    near = jnp.minimum(step, nz - step)
    from_here = step < nz // 2
    place = jnp.where(
        near == 0,
        dx * 2 + dc,
        jnp.where(
            near == nz // 2,
            28 + dc * 2 + dx,
            near * 8 - 4 + jnp.where(from_here, dx * 2 + dc, 5 + dx * 2 - dc),
        ),
    )
    in_group = target % ROWS_G
    even = in_group % 2 == 0
    first = place * block + (in_group // 2) * SLOTS + jnp.where(even, 0, SLOTS - 1)
    turn = jnp.where(even, 1, -1)
    size = per_slab * POS

    table = (me, first, turn, partial_value)
    far = taken(table, (1,))
    behind = taken(table, tuple(range(2, 8)))
    beyond = taken(table, (8,))[0]
    own = taken(table, (9,))[0]
    far = paired(table, 0, other_core(far), 0)
    far = onward(far, "y")
    behind = other_core(behind)
    across = lax.ppermute(beyond, "xh", SWAP)
    came = [far, far]
    for step, k in enumerate((3, 2, 1)):
        for v in range(2):
            total = paired(
                table, 8 + 2 * k + v, behind, 2 * step + v, came[v], step == 0
            )
            if k == 1 and v == 0:
                came[v] = lax.ppermute(total, (*TP, "c"), diagonal(ny))
            else:
                came[v] = onward(total, "y")
    given = other_core(came[0][1] + came[1][1])
    summed = own + across + came[0][0] + came[1][0] + given

    squares = jnp.sum(summed * summed, axis=1)
    squares = jnp.sum(
        lax.all_to_all(
            jnp.broadcast_to(squares[None], (4 * nz, size)), GRP, 0, 0, tiled=True
        ),
        axis=0,
    )
    inverse = lax.rsqrt(squares / D + EPSILON)
    own_target = lax.dynamic_slice(target, ((xh * ny + y) * per_slab,), (per_slab,))
    own_used = jnp.sum(
        jnp.where(
            own_target[:, None] == jnp.arange(accepted.shape[0], dtype=jnp.int32)[None, :],
            accepted[None, :],
            0,
        ),
        axis=1,
    )
    live = (jnp.arange(POS, dtype=jnp.int32)[None, :] <= own_used[:, None]).reshape(size)
    normed = summed * inverse[:, None] * norm_gain[None, :]
    return jnp.where(live[:, None], normed, jnp.zeros_like(normed)).astype(jnp.bfloat16)


def solution(mesh):
    split = Mesh(mesh.devices.reshape(2, 8, 2, 8, 2), ("xh", "y", "xl", "z", "c"))
    feats, weight = P(GRP, TP), P(TP, GRP)
    return jax.shard_map(
        step_on_device,
        mesh=split,
        in_specs=(feats, feats, feats, weight, weight, weight, P(GRP), P(), P()),
        out_specs=P(TP, GRP),
        check_vma=False,
    )
```

```python
import jax
import jax.numpy as jnp
from jax import lax
from jax.experimental import pallas as pl
from jax.experimental.pallas import tpu as pltpu
from jax.sharding import Mesh
from jax.sharding import PartitionSpec as P

D = 16384
ROWS_G = 8
POS = 6
SLOTS = 8
EPSILON = 1e-05
TP = ("xh", "y")
GRP = ("xl", "z", "c")
SWAP = [(0, 1), (1, 0)]


def both_ways(n):
    pairs = []
    for i in range(n):
        for c in range(2):
            to = (i + (1 if c == 0 else n - 1)) % n
            pairs.append((i * 2 + c, to * 2 + c))
    return pairs


def diagonal(n):
    pairs = []
    for x in range(2):
        for i in range(n):
            for c in range(2):
                to = (i + (1 if c == 0 else n - 1)) % n
                pairs.append(((x * n + i) * 2 + c, ((1 - x) * n + to) * 2 + c))
    return pairs


def other_core(x):
    return lax.ppermute(x, "c", SWAP)


def onward(x, axis):
    return lax.ppermute(x, (axis, "c"), both_ways(lax.axis_size(axis)))


VMEM = pl.BlockSpec(memory_space=pltpu.VMEM)
SMEM = pl.BlockSpec(memory_space=pltpu.SMEM)
HBM = pl.BlockSpec(memory_space=pltpu.HBM)
SMALL = pltpu.CompilerParams(vmem_limit_bytes=8 << 20)


def joined(*parts):
    def kernel(*refs):
        at = 0
        for ref in refs[:-1]:
            refs[-1][at : at + ref.shape[0]] = ref[...]
            at += ref.shape[0]

    shape = (sum(p.shape[0] for p in parts), *parts[0].shape[1:])
    return pl.pallas_call(
        kernel,
        out_shape=jax.ShapeDtypeStruct(shape, parts[0].dtype),
        in_specs=[VMEM] * len(parts),
        out_specs=VMEM,
        compiler_params=SMALL,
        name="joined",
    )(*parts)


def each_row(me, first, turn, values, block, do):
    xh, y, c, ny = me[0], me[1], me[2], 8
    k, v = block // 2 - 4, block % 2
    if k == -4:
        h = jnp.where(c == v, 1 - xh, xh)
    else:
        h = xh if v else 1 - xh
    slab = h * ny + lax.rem(y + (1 - 2 * c) * k + ny, ny)
    per_slab = first.shape[0] // (2 * ny)

    @pl.loop(0, per_slab)
    def _(i):
        start, by = first[slab * per_slab + i], turn[slab * per_slab + i]
        for p in range(POS):
            do(i * POS + p, values[pl.ds(start + by * p, 1), :])


def taken(table, blocks):
    _, first, _, values = table

    def kernel(me, first, turn, values, out):
        for n, block in enumerate(blocks):

            def store(r, row, n=n):
                out[n, pl.ds(r, 1), :] = row

            each_row(me, first, turn, values, block, store)

    return pl.pallas_call(
        kernel,
        out_shape=jax.ShapeDtypeStruct(
            (len(blocks), first.shape[0] // 16 * POS, values.shape[1]), values.dtype
        ),
        in_specs=[SMEM, SMEM, SMEM, VMEM],
        out_specs=VMEM,
        compiler_params=SMALL,
        name="taken",
    )(*table)


def paired(table, block, theirs, at, came=None, first_step=False):
    def kernel(*refs):
        me, first, turn, values, theirs = refs[:5]
        out = refs[-1]

        def store(r, row):
            out[0, pl.ds(r, 1), :] = row

        each_row(me, first, turn, values, block, store)
        if came is None:
            out[1] = theirs[at]
        elif not first_step:
            out[0] = out[0] + refs[5][0]
            out[1] = theirs[at] + refs[5][1]
        else:
            wanted = me[2] == block % 2
            out[0] = out[0] + jnp.where(wanted, refs[5][0], 0.0)
            out[1] = theirs[at] + jnp.where(wanted, refs[5][1], 0.0)

    more = [] if came is None else [came]
    return pl.pallas_call(
        kernel,
        out_shape=jax.ShapeDtypeStruct((2, *theirs.shape[1:]), theirs.dtype),
        in_specs=[SMEM, SMEM, SMEM, VMEM, VMEM, VMEM][: 5 + len(more)],
        out_specs=VMEM,
        compiler_params=SMALL,
        name="paired",
    )(*table, theirs, *more)


def pick_kernel(me, accepted, low, mid, high, out, used_by, held, sems):
    feats = (low, mid, high)
    copies = [pltpu.make_async_copy(accepted, used_by, sems.at[3])]
    copies += [pltpu.make_async_copy(f, held.at[i], sems.at[i]) for i, f in enumerate(feats)]
    for copy in copies:
        copy.start()
    slots, (tokens, k) = out.shape[0], low.shape
    slot = lax.broadcasted_iota(jnp.int32, (slots, tokens), 0)
    token = lax.broadcasted_iota(jnp.int32, (slots, tokens), 1)
    pair, at = slot // SLOTS, slot % SLOTS
    used = jnp.zeros_like(slot)
    copies[0].wait()
    for i in range(ROWS_G // 2):
        used = jnp.where(pair == i, used_by[me[3] * ROWS_G + 2 * i] + 1, used)
    source = pair * (2 * POS) + jnp.where(at < used, at, 2 * POS + 1 - at)
    pick = jnp.where(source == token, 1.0, 0.0).astype(jnp.bfloat16)
    for i in range(3):
        copies[1 + i].wait()
        out[:, i * k : (i + 1) * k] = jnp.dot(
            pick, held[i], preferred_element_type=jnp.float32
        ).astype(jnp.bfloat16)


def selected(feats, me, accepted):
    slots, width = ROWS_G // 2 * SLOTS, 3 * feats[0].shape[1]
    return pl.pallas_call(
        pick_kernel,
        out_shape=jax.ShapeDtypeStruct((slots, width), jnp.bfloat16),
        in_specs=[SMEM] + [HBM] * 4,
        out_specs=VMEM,
        scratch_shapes=[
            pltpu.SMEM(accepted.shape, jnp.int32),
            pltpu.VMEM((3, *feats[0].shape), jnp.bfloat16),
            pltpu.SemaphoreType.DMA((4,)),
        ],
        compiler_params=SMALL,
        name="pick",
    )(me, *(pltpu.with_memory_space_constraint(x, pltpu.HBM) for x in (accepted, *feats)))


def product(parts, weights, rows, at, before=None):
    columns = weights[0].shape[1]
    count = sum(n for _, _, n in parts)
    arrays = []
    for p, _, _ in parts:
        if not any(p is q for q in arrays):
            arrays.append(p)
    which = [next(i for i, q in enumerate(arrays) if q is p) for p, _, _ in parts]
    depth = arrays[0].shape[1]

    def kernel(*refs):
        n = len(arrays)
        if before is None:
            out, near, held, sems = refs[-4:]
            k = depth // 3
            copies = [
                pltpu.make_async_copy(refs[n + i], near.at[pl.ds(i * k, k)], sems.at[i])
                for i in range(3)
            ]
            for copy in copies:
                copy.start()
        else:
            near, (out, _, held) = refs[n], refs[-3:]
        to = 0
        for i, (_, start, number) in zip(which, parts, strict=True):
            held[to : to + number] = refs[i][start : start + number]
            to += number
        if before is None:
            for copy in copies:
                copy.wait()
        out[at : at + count] = jnp.dot(
            held[...], near[...], preferred_element_type=jnp.float32
        )

    if before is None:
        weights = [pltpu.with_memory_space_constraint(w, pltpu.HBM) for w in weights]
    operands = arrays + list(weights)
    aliases = {} if before is None else {len(operands): 0, len(arrays): 1}
    shapes = (
        jax.ShapeDtypeStruct((rows, columns), jnp.float32),
        jax.ShapeDtypeStruct((depth, columns), jnp.bfloat16),
    )
    return pl.pallas_call(
        kernel,
        out_shape=shapes,
        in_specs=[VMEM] * len(arrays) + ([HBM] * 3 if before is None else [VMEM] * 2),
        out_specs=(VMEM,) * len(shapes),
        scratch_shapes=[pltpu.VMEM((count, depth), jnp.bfloat16)]
        + ([pltpu.SemaphoreType.DMA((3,))] if before is None else []),
        input_output_aliases=aliases,
        compiler_params=pltpu.CompilerParams(vmem_limit_bytes=6 << 20),
        name="product",
    )(*operands, *([] if before is None else [before]))


def step_on_device(
    low_feats, mid_feats, high_feats, w_low, w_mid, w_high, norm_gain, accepted, assignment
):
    weights = (w_low, w_mid, w_high)
    xh, y, xl, z, c = (lax.axis_index(a) for a in ("xh", "y", "xl", "z", "c"))
    ny, nz = lax.axis_size("y"), lax.axis_size("z")
    back = 2 * c - 1
    group = (xl * nz + z) * 2 + c
    me = jnp.stack([xh, y, c, group, back])
    mine = selected((low_feats, mid_feats, high_feats), me, accepted)
    block = mine.shape[0]

    chip = joined(mine, other_core(mine))
    straight = [onward(chip, "z")]
    crossed = [lax.ppermute(chip, GRP, diagonal(nz))]
    beside = lax.ppermute(mine, "xl", SWAP)
    for _ in range(2):
        straight.append(onward(straight[-1], "z"))
        crossed.append(onward(crossed[-1], "z"))
    straight.append(onward(straight[-1], "z"))
    crossed.append(onward(crossed[-1], "z"))
    here, there = [], []
    for s in range(3):
        here.append(joined(straight[s], crossed[s], *((beside,) if s == 1 else ())))
        there.append(other_core(here[s]))
    cut = 4 * block
    total = 32 * block
    partial_value, near = product([(chip, 0, 2 * block)], weights, total, 0)
    parts = [
        (beside, 0, block),
        (there[1], cut, block),
        (here[0], 0, cut),
        (there[0], 0, cut),
        (here[1], 0, cut),
        (there[1], 0, cut),
    ]
    partial_value, near = product(parts, (near,), total, 2 * block, partial_value)
    parts = [(here[2], 0, cut), (there[2], 0, cut)]
    partial_value, near = product(parts, (near,), total, 20 * block, partial_value)
    parts = [(straight[3], 0, 2 * block), (crossed[3], 0, 2 * block)]
    partial_value, near = product(parts, (near,), total, 28 * block, partial_value)

    per_slab = assignment.shape[0] // (2 * ny)
    target = assignment
    of_group = target // ROWS_G
    there_c, there_z, there_x = of_group % 2, (of_group // 2) % nz, of_group // (2 * nz)
    dx, dc, dz = there_x ^ xl, there_c ^ c, (there_z - z) % nz
    step = (nz + back * dz) % nz
    near = jnp.minimum(step, nz - step)
    from_here = step < nz // 2
    place = jnp.where(
        near == 0,
        dx * 2 + dc,
        jnp.where(
            near == nz // 2,
            28 + dx * 2 + dc,
            near * 8 - 4 + jnp.where(from_here, dx * 2 + dc, 5 + dx * 2 - dc),
        ),
    )
    in_group = target % ROWS_G
    even = in_group % 2 == 0
    first = place * block + (in_group // 2) * SLOTS + jnp.where(even, 0, SLOTS - 1)
    turn = jnp.where(even, 1, -1)
    size = per_slab * POS

    table = (me, first, turn, partial_value)
    far = taken(table, (1,))
    behind = taken(table, tuple(range(2, 8)))
    beyond = taken(table, (8,))[0]
    own = taken(table, (9,))[0]
    far = paired(table, 0, other_core(far), 0)
    far = onward(far, "y")
    behind = other_core(behind)
    across = lax.ppermute(beyond, "xh", SWAP)
    came = [far, far]
    for step, k in enumerate((3, 2, 1)):
        for v in range(2):
            total = paired(
                table, 8 + 2 * k + v, behind, 2 * step + v, came[v], step == 0
            )
            if k == 1 and v == 0:
                came[v] = lax.ppermute(total, (*TP, "c"), diagonal(ny))
            else:
                came[v] = onward(total, "y")
    given = other_core(came[0][1] + came[1][1])
    summed = own + across + came[0][0] + came[1][0] + given

    squares = jnp.sum(summed * summed, axis=1)
    squares = jnp.sum(
        lax.all_to_all(
            jnp.broadcast_to(squares[None], (4 * nz, size)), GRP, 0, 0, tiled=True
        ),
        axis=0,
    )
    inverse = lax.rsqrt(squares / D + EPSILON)
    own_target = lax.dynamic_slice(target, ((xh * ny + y) * per_slab,), (per_slab,))
    own_used = jnp.sum(
        jnp.where(
            own_target[:, None] == jnp.arange(accepted.shape[0], dtype=jnp.int32)[None, :],
            accepted[None, :],
            0,
        ),
        axis=1,
    )
    live = (jnp.arange(POS, dtype=jnp.int32)[None, :] <= own_used[:, None]).reshape(size)
    normed = summed * inverse[:, None] * norm_gain[None, :]
    return jnp.where(live[:, None], normed, jnp.zeros_like(normed)).astype(jnp.bfloat16)


def solution(mesh):
    split = Mesh(mesh.devices.reshape(2, 8, 2, 8, 2), ("xh", "y", "xl", "z", "c"))
    feats, weight = P(GRP, TP), P(TP, GRP)
    return jax.shard_map(
        step_on_device,
        mesh=split,
        in_specs=(feats, feats, feats, weight, weight, weight, P(GRP), P(), P()),
        out_specs=P(TP, GRP),
        check_vma=False,
    )
```

```python
import jax
import jax.numpy as jnp
from jax import lax
from jax.experimental import pallas as pl
from jax.experimental.pallas import tpu as pltpu
from jax.sharding import Mesh
from jax.sharding import PartitionSpec as P

D = 16384
ROWS_G = 8
POS = 6
SLOTS = 8
EPSILON = 1e-05
TP = ("xh", "y")
GRP = ("xl", "z", "c")
SWAP = [(0, 1), (1, 0)]


def both_ways(n):
    pairs = []
    for i in range(n):
        for c in range(2):
            to = (i + (1 if c == 0 else n - 1)) % n
            pairs.append((i * 2 + c, to * 2 + c))
    return pairs


def diagonal(n):
    pairs = []
    for x in range(2):
        for i in range(n):
            for c in range(2):
                to = (i + (1 if c == 0 else n - 1)) % n
                pairs.append(((x * n + i) * 2 + c, ((1 - x) * n + to) * 2 + c))
    return pairs


def other_core(x):
    return lax.ppermute(x, "c", SWAP)


def onward(x, axis):
    return lax.ppermute(x, (axis, "c"), both_ways(lax.axis_size(axis)))


VMEM = pl.BlockSpec(memory_space=pltpu.VMEM)
SMEM = pl.BlockSpec(memory_space=pltpu.SMEM)
HBM = pl.BlockSpec(memory_space=pltpu.HBM)
SMALL = pltpu.CompilerParams(vmem_limit_bytes=8 << 20)


def joined(*parts):
    def kernel(*refs):
        at = 0
        for ref in refs[:-1]:
            refs[-1][at : at + ref.shape[0]] = ref[...]
            at += ref.shape[0]

    shape = (sum(p.shape[0] for p in parts), *parts[0].shape[1:])
    return pl.pallas_call(
        kernel,
        out_shape=jax.ShapeDtypeStruct(shape, parts[0].dtype),
        in_specs=[VMEM] * len(parts),
        out_specs=VMEM,
        compiler_params=SMALL,
        name="joined",
    )(*parts)


def each_row(me, first, turn, values, block, do):
    xh, y, c, ny = me[0], me[1], me[2], 8
    k, v = block // 2 - 4, block % 2
    if k == -4:
        h = jnp.where(c == v, 1 - xh, xh)
    else:
        h = xh if v else 1 - xh
    slab = h * ny + lax.rem(y + (1 - 2 * c) * k + ny, ny)
    per_slab = first.shape[0] // (2 * ny)

    @pl.loop(0, per_slab)
    def _(i):
        start, by = first[slab * per_slab + i], turn[slab * per_slab + i]
        for p in range(POS):
            do(i * POS + p, values[pl.ds(start + by * p, 1), :])


def taken(table, blocks):
    _, first, _, values = table

    def kernel(me, first, turn, values, out):
        for n, block in enumerate(blocks):

            def store(r, row, n=n):
                out[n, pl.ds(r, 1), :] = row

            each_row(me, first, turn, values, block, store)

    return pl.pallas_call(
        kernel,
        out_shape=jax.ShapeDtypeStruct(
            (len(blocks), first.shape[0] // 16 * POS, values.shape[1]), values.dtype
        ),
        in_specs=[SMEM, SMEM, SMEM, VMEM],
        out_specs=VMEM,
        compiler_params=SMALL,
        name="taken",
    )(*table)


def paired(table, block, theirs, at, came=None, first_step=False):
    def kernel(*refs):
        me, first, turn, values, theirs = refs[:5]
        out = refs[-1]

        def store(r, row):
            out[0, pl.ds(r, 1), :] = row

        each_row(me, first, turn, values, block, store)
        if came is None:
            out[1] = theirs[at]
        elif not first_step:
            out[0] = out[0] + refs[5][0]
            out[1] = theirs[at] + refs[5][1]
        else:
            wanted = me[2] == block % 2
            out[0] = out[0] + jnp.where(wanted, refs[5][0], 0.0)
            out[1] = theirs[at] + jnp.where(wanted, refs[5][1], 0.0)

    more = [] if came is None else [came]
    return pl.pallas_call(
        kernel,
        out_shape=jax.ShapeDtypeStruct((2, *theirs.shape[1:]), theirs.dtype),
        in_specs=[SMEM, SMEM, SMEM, VMEM, VMEM, VMEM][: 5 + len(more)],
        out_specs=VMEM,
        compiler_params=SMALL,
        name="paired",
    )(*table, theirs, *more)


def pick_kernel(me, accepted, low, mid, high, out, used_by, held, sems):
    feats = (low, mid, high)
    copies = [pltpu.make_async_copy(accepted, used_by, sems.at[3])]
    copies += [pltpu.make_async_copy(f, held.at[i], sems.at[i]) for i, f in enumerate(feats)]
    for copy in copies:
        copy.start()
    slots, (tokens, k) = out.shape[0], low.shape
    slot = lax.broadcasted_iota(jnp.int32, (slots, tokens), 0)
    token = lax.broadcasted_iota(jnp.int32, (slots, tokens), 1)
    pair, at = slot // SLOTS, slot % SLOTS
    used = jnp.zeros_like(slot)
    copies[0].wait()
    for i in range(ROWS_G // 2):
        used = jnp.where(pair == i, used_by[me[3] * ROWS_G + 2 * i] + 1, used)
    source = pair * (2 * POS) + jnp.where(at < used, at, 2 * POS + 1 - at)
    pick = jnp.where(source == token, 1.0, 0.0).astype(jnp.bfloat16)
    for i in range(3):
        copies[1 + i].wait()
        out[:, i * k : (i + 1) * k] = jnp.dot(
            pick, held[i], preferred_element_type=jnp.float32
        ).astype(jnp.bfloat16)


def selected(feats, me, accepted):
    slots, width = ROWS_G // 2 * SLOTS, 3 * feats[0].shape[1]
    return pl.pallas_call(
        pick_kernel,
        out_shape=jax.ShapeDtypeStruct((slots, width), jnp.bfloat16),
        in_specs=[SMEM] + [HBM] * 4,
        out_specs=VMEM,
        scratch_shapes=[
            pltpu.SMEM(accepted.shape, jnp.int32),
            pltpu.VMEM((3, *feats[0].shape), jnp.bfloat16),
            pltpu.SemaphoreType.DMA((4,)),
        ],
        compiler_params=SMALL,
        name="pick",
    )(me, *(pltpu.with_memory_space_constraint(x, pltpu.HBM) for x in (accepted, *feats)))


def product(parts, weights, rows, at, before=None):
    columns = weights[0].shape[1]
    count = sum(n for _, _, n in parts)
    arrays = []
    for p, _, _ in parts:
        if not any(p is q for q in arrays):
            arrays.append(p)
    which = [next(i for i, q in enumerate(arrays) if q is p) for p, _, _ in parts]
    depth = arrays[0].shape[1]

    def kernel(*refs):
        n = len(arrays)
        if before is None:
            out, near, held, sems = refs[-4:]
            k = depth // 3
            copies = [
                pltpu.make_async_copy(refs[n + i], near.at[pl.ds(i * k, k)], sems.at[i])
                for i in range(3)
            ]
            for copy in copies:
                copy.start()
        else:
            near, (out, _, held) = refs[n], refs[-3:]
        to = 0
        for i, (_, start, number) in zip(which, parts, strict=True):
            held[to : to + number] = refs[i][start : start + number]
            to += number
        if before is None:
            for copy in copies:
                copy.wait()
        out[at : at + count] = jnp.dot(
            held[...], near[...], preferred_element_type=jnp.float32
        )

    if before is None:
        weights = [pltpu.with_memory_space_constraint(w, pltpu.HBM) for w in weights]
    operands = arrays + list(weights)
    aliases = {} if before is None else {len(operands): 0, len(arrays): 1}
    shapes = (
        jax.ShapeDtypeStruct((rows, columns), jnp.float32),
        jax.ShapeDtypeStruct((depth, columns), jnp.bfloat16),
    )
    return pl.pallas_call(
        kernel,
        out_shape=shapes,
        in_specs=[VMEM] * len(arrays) + ([HBM] * 3 if before is None else [VMEM] * 2),
        out_specs=(VMEM,) * len(shapes),
        scratch_shapes=[pltpu.VMEM((count, depth), jnp.bfloat16)]
        + ([pltpu.SemaphoreType.DMA((3,))] if before is None else []),
        input_output_aliases=aliases,
        compiler_params=pltpu.CompilerParams(vmem_limit_bytes=6 << 20),
        name="product",
    )(*operands, *([] if before is None else [before]))


def step_on_device(
    low_feats, mid_feats, high_feats, w_low, w_mid, w_high, norm_gain, accepted, assignment
):
    weights = (w_low, w_mid, w_high)
    xh, y, xl, z, c = (lax.axis_index(a) for a in ("xh", "y", "xl", "z", "c"))
    ny, nz = lax.axis_size("y"), lax.axis_size("z")
    back = 2 * c - 1
    group = (xl * nz + z) * 2 + c
    me = jnp.stack([xh, y, c, group, back])
    mine = selected((low_feats, mid_feats, high_feats), me, accepted)
    block = mine.shape[0]

    chip = joined(mine, other_core(mine))
    straight = [onward(chip, "z")]
    crossed = [lax.ppermute(chip, GRP, diagonal(nz))]
    beside = lax.ppermute(mine, "xl", SWAP)
    for _ in range(2):
        straight.append(onward(straight[-1], "z"))
        crossed.append(onward(crossed[-1], "z"))
    straight.append(onward(straight[-1], "z"))
    crossed.append(onward(crossed[-1], "z"))
    here, there = [], []
    for s in range(3):
        here.append(joined(straight[s], crossed[s], *((beside,) if s == 1 else ())))
        there.append(other_core(here[s]))
    cut = 4 * block
    total = 32 * block
    partial_value, near = product([(chip, 0, 2 * block)], weights, total, 0)
    parts = [
        (beside, 0, block),
        (there[1], cut, block),
        (here[0], 0, cut),
        (there[0], 0, cut),
        (here[1], 0, cut),
        (there[1], 0, cut),
    ]
    partial_value, near = product(parts, (near,), total, 2 * block, partial_value)
    parts = [(here[2], 0, cut), (there[2], 0, cut)]
    partial_value, near = product(parts, (near,), total, 20 * block, partial_value)
    parts = [(straight[3], 0, 2 * block), (crossed[3], 0, 2 * block)]
    partial_value, near = product(parts, (near,), total, 28 * block, partial_value)

    per_slab = assignment.shape[0] // (2 * ny)
    target = assignment
    of_group = target // ROWS_G
    there_c, there_z, there_x = of_group % 2, (of_group // 2) % nz, of_group // (2 * nz)
    dx, dc, dz = there_x ^ xl, there_c ^ c, (there_z - z) % nz
    step = (nz + back * dz) % nz
    near = jnp.minimum(step, nz - step)
    from_here = step < nz // 2
    place = jnp.where(
        near == 0,
        dx * 2 + dc,
        jnp.where(
            near == nz // 2,
            28 + dx * 2 + dc,
            near * 8 - 4 + jnp.where(from_here, dx * 2 + dc, 5 + dx * 2 - dc),
        ),
    )
    in_group = target % ROWS_G
    even = in_group % 2 == 0
    first = place * block + (in_group // 2) * SLOTS + jnp.where(even, 0, SLOTS - 1)
    turn = jnp.where(even, 1, -1)
    size = per_slab * POS

    table = (me, first, turn, partial_value)
    far = taken(table, (1,))
    soon = taken(table, (2, 3))
    behind = taken(table, tuple(range(4, 8)))
    beyond = taken(table, (8,))[0]
    own = taken(table, (9,))[0]
    far = paired(table, 0, other_core(far), 0)
    far = onward(far, "y")
    soon = other_core(soon)
    behind = other_core(behind)
    across = lax.ppermute(beyond, "xh", SWAP)
    came = [far, far]
    for step, k in enumerate((3, 2, 1)):
        for v in range(2):
            total = paired(
                table,
                8 + 2 * k + v,
                behind if step else soon,
                2 * max(step - 1, 0) + v,
                came[v],
                step == 0,
            )
            if k == 1 and v == 0:
                came[v] = lax.ppermute(total, (*TP, "c"), diagonal(ny))
            else:
                came[v] = onward(total, "y")
    given = other_core(came[0][1] + came[1][1])
    summed = own + across + came[0][0] + came[1][0] + given

    squares = jnp.sum(summed * summed, axis=1)
    squares = jnp.sum(
        lax.all_to_all(
            jnp.broadcast_to(squares[None], (4 * nz, size)), GRP, 0, 0, tiled=True
        ),
        axis=0,
    )
    inverse = lax.rsqrt(squares / D + EPSILON)
    own_target = lax.dynamic_slice(target, ((xh * ny + y) * per_slab,), (per_slab,))
    own_used = jnp.sum(
        jnp.where(
            own_target[:, None] == jnp.arange(accepted.shape[0], dtype=jnp.int32)[None, :],
            accepted[None, :],
            0,
        ),
        axis=1,
    )
    live = (jnp.arange(POS, dtype=jnp.int32)[None, :] <= own_used[:, None]).reshape(size)
    normed = summed * inverse[:, None] * norm_gain[None, :]
    return jnp.where(live[:, None], normed, jnp.zeros_like(normed)).astype(jnp.bfloat16)


def solution(mesh):
    split = Mesh(mesh.devices.reshape(2, 8, 2, 8, 2), ("xh", "y", "xl", "z", "c"))
    feats, weight = P(GRP, TP), P(TP, GRP)
    return jax.shard_map(
        step_on_device,
        mesh=split,
        in_specs=(feats, feats, feats, weight, weight, weight, P(GRP), P(), P()),
        out_specs=P(TP, GRP),
        check_vma=False,
    )
```
